32 devices in a mesh: scene: 8 (over z, x), tie: 4 (over y, core).
Axes of the slice: x: 2, y: 2, z: 4, core: 2. Of those that a mesh axis runs over, the one named last changes fastest.
Arguments:
- tie_rows: bfloat16 [384, 256, 256], P('tie'), may hold values from -0.375 to 0.375
- point_counts: int32 [384], P('tie'), may hold values from 1 to 128, as said below
- pattern: int32 [128, 384], P('scene', 'tie'), may hold values 0 or 1
- sensitivity: bfloat16 [128, 192, 192], P('scene'), may hold values from -0.119628906 to 0.119628906
- damping: float32 [128], P(('scene', 'tie')), may hold values from 1 to 8
- prior: float32 [64], replicated, may hold values from 0.25 to 4
Outputs:
- scene_rows: float32 [128, 192, 256], P(('scene', 'tie'))
- global_factor: float32 [64, 64], replicated
The draws below stay inside these ranges and needn't reach their ends.
Inputs may be any that keep to these rules, and one draw needn't show every extreme that they name: `point_counts`: points present in each block; some block is full.
All inputs are finite; a program needn't handle non-finite values. No bound on the sum of `pattern` on one device may be relied on, other than what follows from the above.
Results may differ from the reference program's by a relative error of at most 0.0003.
Values sent between devices are 32-bit elements; how exact they have to be, the bound alone decides.
A program may use at most 128 MiB of HBM per device.

```python
import math
import jax
import jax.numpy as jnp
from jax import lax

SPLINE = 192
SHARED = 64
COLS = 256
PTS = 128
ROWS = 256
SC_SHARD = 16
NSC = 128
NBLK = 384
N_SCENE = 8


def draw_point_counts(key, part):
    first_key, second_key = jax.random.split(jax.random.fold_in(key, 11))
    counts = jax.random.randint(first_key, (NBLK,), PTS // 4, PTS + 1)
    chosen = jax.random.randint(second_key, (), 0, NBLK)
    return jnp.where(jnp.arange(NBLK) == chosen, PTS, counts).astype(jnp.int32)


def plant(drawn, key, smallest, top_value):
    spot = [jax.random.randint(jax.random.fold_in(key, axis), (), 0, length) for axis, length in enumerate(drawn.shape)]
    main_axis = drawn.shape.index(max(drawn.shape))
    neighbour = spot[:main_axis] + [(spot[main_axis] + 1) % drawn.shape[main_axis]] + spot[main_axis + 1:]
    return drawn.at[tuple(spot)].set(smallest).at[tuple(neighbour)].set(top_value)


def block_levels(stream_key, extent, pieces, least, largest):
    def one(axis_at, shards_of):
        heights = jax.random.uniform(jax.random.fold_in(jax.random.fold_in(stream_key, 6), axis_at), (shards_of,), jnp.float32, least / len(pieces), largest / len(pieces))
        return jnp.repeat(jnp.exp(heights), extent[axis_at] // shards_of).reshape((-1,) + (1,) * (len(extent) - axis_at - 1))

    gain = one(*pieces[0])
    for cut in pieces[1:]:
        gain = gain * one(*cut)
    return gain


def normal_values(rng, dims, spread, most, pieces=(), kind=jnp.bfloat16):
    result = spread * jax.random.normal(rng, dims, jnp.float32)
    if pieces:
        result = result * block_levels(rng, dims, pieces, -0.22, 0.18)
    return jnp.clip(result, -most, most).astype(kind)


def setup_inputs(seed: int = 0) -> dict:
    key_list = jax.random.split(jax.random.key(seed), 7)
    return {
        "tie_rows": normal_values(key_list[0], (NBLK, ROWS, COLS), ROWS ** -0.5, 0.375, ((0, 4),)),
        "point_counts": draw_point_counts(jax.random.fold_in(key_list[6], 71), 0),
        "pattern": plant((jax.random.randint(key_list[2], (NSC, NBLK), 0, 16) < 1).astype(jnp.int32), jax.random.fold_in(key_list[2], 1), 0, 1),
        "sensitivity": normal_values(key_list[3], (NSC, SPLINE, SPLINE), 0.02, 0.119628906, ((0, 8),)),
        "damping": jnp.clip(jnp.exp(math.log(8.0) - 2.0794415 * jax.random.uniform(key_list[4], (NSC,), jnp.float32) ** block_levels(key_list[4], (NSC,), ((0, 32),), -0.2, 0.2)), 1.0, 8.0),
        "prior": jnp.clip(jnp.exp(jax.random.uniform(key_list[5], (SHARED,), jnp.float32, math.log(0.25), math.log(4.0))), 0.25, 4.0),
    }


highest = lax.Precision.HIGHEST

def block_gram(tie_rows, point_counts):
    row_index = lax.broadcasted_iota(jnp.int32, (tie_rows.shape[0], tie_rows.shape[1]), 1)
    row_valid = (row_index // 2 < point_counts[:, None]).astype(jnp.float32)
    full_rows = tie_rows.astype(jnp.float32)
    masked_rows = full_rows * row_valid[:, :, None]
    return jnp.einsum('brc,brd->bcd', masked_rows, full_rows, precision=highest)

def scene_info(merged, sensitivity, width):
    basis = jnp.eye(width, dtype=jnp.float32)[None] + sensitivity.astype(jnp.float32)
    corner = merged[:, :width, :width]
    side = merged[:, :width, width:]
    tail = merged[:, width:, width:]
    mixed = jnp.einsum('sab,sbc->sac', corner, basis, precision=highest)
    corner_new = jnp.einsum('sba,sbc->sac', basis, mixed, precision=highest)
    side_new = jnp.einsum('sba,sbc->sac', basis, side, precision=highest)
    upper_half = jnp.concatenate([corner_new, side_new], 2)
    lower_half = jnp.concatenate([jnp.transpose(side_new, (0, 2, 1)), tail], 2)
    return jnp.concatenate([upper_half, lower_half], 1)

def factor_scenes(information, damping, width):
    identity = jnp.eye(width, dtype=jnp.float32)
    corner = information[:, :width, :width] + damping[:, None, None] * identity
    chol_lower = jnp.linalg.cholesky(corner)
    cross = jax.scipy.linalg.solve_triangular(chol_lower, information[:, :width, width:], lower=True)
    reduced = information[:, width:, width:] - jnp.einsum('sab,sac->sbc', cross, cross, precision=highest)
    out_rows = jnp.concatenate([jnp.transpose(chol_lower, (0, 2, 1)), cross], 2)
    return (out_rows, jnp.sum(reduced, 0))

def reference(tie_rows, point_counts, pattern, sensitivity, damping, prior):
    block_grams = block_gram(tie_rows, point_counts)
    grams_flat = block_grams.reshape(NBLK, COLS * COLS)

    def group(items):
        group_pattern, group_sens, group_damp = items
        merged = jnp.dot(group_pattern.astype(jnp.float32), grams_flat, precision=highest).reshape(SC_SHARD, COLS, COLS)
        information = scene_info(merged, group_sens, SPLINE)
        return factor_scenes(information, group_damp, SPLINE)
    rows_out, reduced_parts = lax.map(group, (pattern.reshape(N_SCENE, SC_SHARD, NBLK), sensitivity.reshape(N_SCENE, SC_SHARD, SPLINE, SPLINE), damping.reshape(N_SCENE, SC_SHARD)))
    scene_rows = rows_out.reshape(NSC, SPLINE, COLS)
    total = jnp.diag(prior) + jnp.sum(reduced_parts, 0) / NSC
    return (scene_rows, jnp.transpose(jnp.linalg.cholesky(total)))
```

```python
import functools
import math

import jax
import jax.numpy as jnp
from jax import lax
from jax.experimental import pallas as pl
from jax.experimental.pallas import tpu as pltpu
from jax.sharding import PartitionSpec as P

MESH = pl.DeviceIdType.MESH
HIGHEST = lax.Precision.HIGHEST
F32 = jnp.float32
BF16 = jnp.bfloat16
PANEL = 32
LANES = 128
VMEM = pl.BlockSpec(memory_space=pltpu.VMEM)


def over_rows(a, b, precision=None):
    return lax.dot_general(
        a, b, (((0,), (0,)), ((), ())), precision=precision, preferred_element_type=F32
    )


def gram_kernel(chunk, most, counts, order, active, rows_ref, out_ref, gram_ref):
    step = pl.program_id(0)

    @pl.when(step == 0)
    def _():
        out_ref[...] = jnp.zeros_like(out_ref)

    half = rows_ref.shape[2] // 2
    row_index = lax.broadcasted_iota(jnp.int32, rows_ref.shape[1:], 0)
    for i in range(chunk):
        rows = rows_ref[i]
        valid = jnp.where(row_index < 2 * counts[step * chunk + i], 1.0, 0.0).astype(BF16)
        kept = rows * valid
        top = over_rows(kept[:, :half], rows)
        gram_ref[i, :half] = top[:, :half]
        gram_ref[i, half : 2 * half] = top[:, half:]
        gram_ref[i, 2 * half :] = over_rows(kept[:, half:], rows[:, half:])
    for i in range(chunk):
        block = step * chunk + i

        def add(k, carry, i=i, block=block):
            scene = order[block * most + k]
            out_ref[scene] += gram_ref[i]
            return carry

        lax.fori_loop(0, active[block], add, 0)


def merged_partials(tie_rows, point_counts, pattern):
    blocks, rows, width = tie_rows.shape
    scenes = pattern.shape[0]
    half = width // 2
    chunk = math.gcd(blocks, 8)
    index = jnp.arange(scenes)
    seen = (pattern != 0).astype(jnp.int32).T
    before = jnp.sum(seen[:, None, :] * (index[None, :] < index[:, None])[None], 2)
    hits = (before[:, :, None] == index) & (seen[:, :, None] != 0)
    order = jnp.sum(jnp.where(hits, index[None, :, None], 0), 1).reshape(-1)
    return pl.pallas_call(
        functools.partial(gram_kernel, chunk, scenes),
        grid_spec=pltpu.PrefetchScalarGridSpec(
            num_scalar_prefetch=3,
            grid=(blocks // chunk,),
            in_specs=[pl.BlockSpec((chunk, rows, width), lambda i, *_: (i, 0, 0))],
            out_specs=pl.BlockSpec((scenes, 3 * half, half), lambda i, *_: (0, 0, 0)),
            scratch_shapes=[pltpu.VMEM((chunk, 3 * half, half), F32)],
        ),
        out_shape=jax.ShapeDtypeStruct((scenes, 3 * half, half), F32),
        name="grams",
    )(point_counts, order.astype(jnp.int32), jnp.sum(seen, 1), tie_rows)


def scatter_kernel(n, own, part, out, got, summed, far, s1, r1, s2, r2):
    me = lax.axis_index("tie")
    pairs = n // 2
    parity = lax.rem(me, 2)
    group = me // 2
    partner = me + 1 - 2 * parity

    def member(k, side):
        return lax.rem(group + k, pairs) * 2 + side

    barrier = pltpu.get_barrier_semaphore()
    pl.semaphore_signal(barrier, inc=1, device_id={"tie": partner}, device_id_type=MESH)
    for k in range(1, pairs):
        pl.semaphore_signal(
            barrier, inc=1, device_id={"tie": member(k, parity)}, device_id_type=MESH
        )
    pl.semaphore_wait(barrier, pairs)

    order = [(k, q) for k in list(range(1, pairs)) + [0] for q in range(own)]
    first, second = {}, {}
    for k, q in order:
        slot = k * own + q
        first[k, q] = pltpu.make_async_remote_copy(
            src_ref=part.at[member(k, 1 - parity) * own + q],
            dst_ref=got.at[slot],
            send_sem=s1.at[slot],
            recv_sem=r1.at[slot],
            device_id={"tie": partner},
            device_id_type=MESH,
        )
        first[k, q].start()
    for k, q in order:
        slot = k * own + q
        first[k, q].wait_recv()
        mine = member(k, parity) * own + q
        if k == 0:
            out[q] = part[mine] + got[slot]
        else:
            summed[slot] = part[mine] + got[slot]
            second[k, q] = pltpu.make_async_remote_copy(
                src_ref=summed.at[slot],
                dst_ref=far.at[slot],
                send_sem=s2.at[slot],
                recv_sem=r2.at[slot],
                device_id={"tie": member(k, parity)},
                device_id_type=MESH,
            )
            second[k, q].start()
    for k, q in order:
        if k:
            second[k, q].wait_recv()
            out[q] += far[k * own + q]
    for k, q in order:
        first[k, q].wait_send()
        if k:
            second[k, q].wait_send()


def scatter_sum(partials, n):
    scenes, high, wide = partials.shape
    own = scenes // n
    slots = own * (n // 2)
    block = (slots, high, wide)
    dma = pltpu.SemaphoreType.DMA((slots,))
    return pl.pallas_call(
        functools.partial(scatter_kernel, n, own),
        out_shape=jax.ShapeDtypeStruct((own, high, wide), F32),
        in_specs=[VMEM],
        out_specs=VMEM,
        scratch_shapes=[pltpu.VMEM(block, F32)] * 3 + [dma] * 4,
        compiler_params=pltpu.CompilerParams(collective_id=0, has_side_effects=True),
        name="scatter",
    )(partials)


def three_parts(x):
    high = x.astype(BF16)
    rest = x - high.astype(F32)
    middle = rest.astype(BF16)
    return high, middle, (rest - middle.astype(F32)).astype(BF16)


def eliminate(panels, first_column):
    shape = panels[0].shape
    row_index = lax.broadcasted_iota(jnp.int32, shape, 0)
    lane = lax.broadcasted_iota(jnp.int32, shape, 1)
    for j in range(shape[0]):
        c = first_column + j
        for q, panel in enumerate(panels):
            column = jnp.broadcast_to(panel[:, c : c + 1], shape)
            scaled = panel[j : j + 1] / column[j : j + 1]
            panels[q] = panel - jnp.where(row_index > j, column, 0.0) * scaled
    above = lane >= row_index + first_column
    on_diagonal = lane == row_index + first_column
    done = []
    for panel in panels:
        diagonal = jnp.sum(jnp.where(on_diagonal, panel, 0.0), 1, keepdims=True)
        root = jnp.broadcast_to(jnp.sqrt(diagonal), shape)
        done.append(jnp.where(above, panel / root, 0.0))
    return done


def factor_kernel(damping, merged, sens, out, reduced, info):
    own, width, _ = info.shape
    spline = out.shape[1]
    half = width // 2
    row_index = lax.broadcasted_iota(jnp.int32, (width, width), 0)
    lane = lax.broadcasted_iota(jnp.int32, (width, width), 1)
    on_diagonal = (row_index == lane) & (row_index < spline)
    for q in range(own):
        side = merged[q, half : 2 * half]
        top = jnp.concatenate([merged[q, :half], side], 1)
        bottom = jnp.concatenate([side.T, merged[q, 2 * half :]], 1)
        whole = jnp.concatenate([top, bottom], 0)
        s = sens[q]
        mixed = whole
        for piece in three_parts(whole):
            mixed = mixed + jnp.dot(piece, s, preferred_element_type=F32)
        result = mixed + over_rows(s.astype(F32), mixed, HIGHEST)
        info[q] = result + jnp.where(on_diagonal, damping[q], 0.0)
    for start in range(0, spline, PANEL):
        base = start // LANES * LANES
        panels = [info[q, start : start + PANEL, base:] for q in range(own)]
        rows = eliminate(panels, start - base)
        for q in range(own):
            out[q, start : start + PANEL, base:] = rows[q]
        if base:
            out[:, start : start + PANEL, :base] = jnp.zeros((own, PANEL, base), F32)
        after = start + PANEL
        for q in range(own):
            info[q, after:, base:] -= over_rows(
                rows[q], rows[q], HIGHEST
            )[after - base :]
    total = info[0, spline:, half:]
    for q in range(1, own):
        total = total + info[q, spline:, half:]
    reduced[...] = total


def factor_scenes(merged, sensitivity, damping, width):
    own = damping.shape[0]
    spline = sensitivity.shape[1]
    half = width // 2
    mine = lax.dynamic_slice_in_dim(sensitivity, lax.axis_index("tie") * own, own)
    beyond = width - spline
    mine = jnp.pad(mine, ((0, 0), (0, beyond), (0, beyond)))
    return pl.pallas_call(
        factor_kernel,
        in_specs=[pl.BlockSpec(memory_space=pltpu.SMEM), VMEM, VMEM],
        out_specs=[VMEM, VMEM],
        scratch_shapes=[pltpu.VMEM((own, width, width), F32)],
        out_shape=[
            jax.ShapeDtypeStruct((own, spline, width), F32),
            jax.ShapeDtypeStruct((width - spline, half), F32),
        ],
        name="factor",
    )(damping, merged, mine)


def total_kernel(axes, x, out, *scratch):
    barrier = pltpu.get_barrier_semaphore()
    for name, n in axes:
        me = lax.axis_index(name)
        for k in range(1, n):
            pl.semaphore_signal(
                barrier, inc=1, device_id={name: lax.rem(me + k, n)}, device_id_type=MESH
            )
    pl.semaphore_wait(barrier, sum(n - 1 for _, n in axes))
    value = x
    for at, (name, n) in enumerate(axes):
        slots, send, recv = scratch[3 * at : 3 * at + 3]
        me = lax.axis_index(name)
        slots[0] = value[...]
        copies = []
        for k in range(1, n):
            copies.append(
                pltpu.make_async_remote_copy(
                    src_ref=slots.at[0],
                    dst_ref=slots.at[k],
                    send_sem=send.at[k],
                    recv_sem=recv.at[k],
                    device_id={name: lax.rem(me + k, n)},
                    device_id_type=MESH,
                )
            )
            copies[-1].start()
        for copy in copies:
            copy.wait_recv()
        acc = slots[me]
        for i in range(1, n):
            acc = acc + slots[lax.rem(me - i + n, n)]
        for copy in copies:
            copy.wait_send()
        out[...] = acc
        value = out


def total_sum(x, axes):
    scratch = []
    for _, n in axes:
        scratch += [pltpu.VMEM((n,) + x.shape, F32)]
        scratch += [pltpu.SemaphoreType.DMA((n,))] * 2
    return pl.pallas_call(
        functools.partial(total_kernel, axes),
        out_shape=jax.ShapeDtypeStruct(x.shape, F32),
        in_specs=[VMEM],
        out_specs=VMEM,
        scratch_shapes=scratch,
        compiler_params=pltpu.CompilerParams(collective_id=1, has_side_effects=True),
        name="total",
    )(x)


def last_kernel(scale, x, prior, out):
    shared, wide = x.shape
    lane = lax.broadcasted_iota(jnp.int32, (shared, wide), 1)
    row = lax.broadcasted_iota(jnp.int32, (shared, wide), 0) + wide - shared
    value = x[...] * scale + jnp.where(lane == row, prior[...], 0.0)
    out[...] = eliminate([value], wide - shared)[0][:, wide - shared :]


def last_factor(x, prior, scale):
    shared = x.shape[0]
    return pl.pallas_call(
        functools.partial(last_kernel, scale),
        out_shape=jax.ShapeDtypeStruct((shared, shared), F32),
        in_specs=[VMEM, VMEM],
        out_specs=VMEM,
        name="last",
    )(x, prior[:, None])


def on_device(axes, tie_rows, point_counts, pattern, sensitivity, damping, prior):
    sizes = dict(axes)
    width = tie_rows.shape[2]
    partials = merged_partials(tie_rows, point_counts, pattern)
    merged = scatter_sum(partials, sizes["tie"])
    scene_rows, reduced = factor_scenes(merged, sensitivity, damping, width)
    total = total_sum(reduced, axes)
    scenes = damping.shape[0] * math.prod(sizes.values())
    return scene_rows, last_factor(total, prior, 1.0 / scenes)


def solution(mesh):
    axes = (("tie", mesh.shape["tie"]), ("scene", mesh.shape["scene"]))
    placed = (
        P("tie", None, None),
        P("tie"),
        P("scene", "tie"),
        P("scene", None, None),
        P(("scene", "tie")),
        P(),
    )
    return jax.shard_map(
        functools.partial(on_device, axes),
        mesh=mesh,
        in_specs=placed,
        out_specs=(P(("scene", "tie"), None, None), P()),
        check_vma=False,
    )
```

```python
import functools
import math

import jax
import jax.numpy as jnp
from jax import lax
from jax.experimental import pallas as pl
from jax.experimental.pallas import tpu as pltpu
from jax.sharding import PartitionSpec as P

MESH = pl.DeviceIdType.MESH
HIGHEST = lax.Precision.HIGHEST
F32 = jnp.float32
BF16 = jnp.bfloat16
PANEL = 32
LANES = 128
VMEM = pl.BlockSpec(memory_space=pltpu.VMEM)


def over_rows(a, b, precision=None):
    return lax.dot_general(
        a, b, (((0,), (0,)), ((), ())), precision=precision, preferred_element_type=F32
    )


def gram_kernel(chunk, most, counts, order, active, rows_ref, out_ref, gram_ref):
    step = pl.program_id(0)

    @pl.when(step == 0)
    def _():
        out_ref[...] = jnp.zeros_like(out_ref)

    half = rows_ref.shape[2] // 2
    row_index = lax.broadcasted_iota(jnp.int32, rows_ref.shape[1:], 0)
    for i in range(chunk):
        rows = rows_ref[i]
        valid = jnp.where(row_index < 2 * counts[step * chunk + i], 1.0, 0.0).astype(BF16)
        kept = rows * valid
        top = over_rows(kept[:, :half], rows)
        gram_ref[i, :half] = top[:, :half]
        gram_ref[i, half : 2 * half] = top[:, half:]
        gram_ref[i, 2 * half :] = over_rows(kept[:, half:], rows[:, half:])
    for i in range(chunk):
        block = step * chunk + i

        def add(k, carry, i=i, block=block):
            scene = order[block * most + k]
            out_ref[scene] += gram_ref[i]
            return carry

        lax.fori_loop(0, active[block], add, 0)


def merged_partials(tie_rows, point_counts, pattern):
    blocks, rows, width = tie_rows.shape
    scenes = pattern.shape[0]
    half = width // 2
    chunk = math.gcd(blocks, 8)
    index = jnp.arange(scenes)
    seen = (pattern != 0).astype(jnp.int32).T
    before = jnp.sum(seen[:, None, :] * (index[None, :] < index[:, None])[None], 2)
    hits = (before[:, :, None] == index) & (seen[:, :, None] != 0)
    order = jnp.sum(jnp.where(hits, index[None, :, None], 0), 1).reshape(-1)
    return pl.pallas_call(
        functools.partial(gram_kernel, chunk, scenes),
        grid_spec=pltpu.PrefetchScalarGridSpec(
            num_scalar_prefetch=3,
            grid=(blocks // chunk,),
            in_specs=[pl.BlockSpec((chunk, rows, width), lambda i, *_: (i, 0, 0))],
            out_specs=pl.BlockSpec((scenes, 3 * half, half), lambda i, *_: (0, 0, 0)),
            scratch_shapes=[pltpu.VMEM((chunk, 3 * half, half), F32)],
        ),
        out_shape=jax.ShapeDtypeStruct((scenes, 3 * half, half), F32),
        name="grams",
    )(point_counts, order.astype(jnp.int32), jnp.sum(seen, 1), tie_rows)


def scatter_kernel(n, own, part, out, got, summed, far, s1, r1, s2, r2):
    me = lax.axis_index("tie")
    pairs = n // 2
    parity = lax.rem(me, 2)
    group = me // 2
    partner = me + 1 - 2 * parity

    def member(k, side):
        return lax.rem(group + k, pairs) * 2 + side

    barrier = pltpu.get_barrier_semaphore()
    pl.semaphore_signal(barrier, inc=1, device_id={"tie": partner}, device_id_type=MESH)
    for k in range(1, pairs):
        pl.semaphore_signal(
            barrier, inc=1, device_id={"tie": member(k, parity)}, device_id_type=MESH
        )
    pl.semaphore_wait(barrier, pairs)

    order = [(k, q) for k in list(range(1, pairs)) + [0] for q in range(own)]
    first, second = {}, {}
    for k, q in order:
        slot = k * own + q
        first[k, q] = pltpu.make_async_remote_copy(
            src_ref=part.at[member(k, 1 - parity) * own + q],
            dst_ref=got.at[slot],
            send_sem=s1.at[slot],
            recv_sem=r1.at[slot],
            device_id={"tie": partner},
            device_id_type=MESH,
        )
        first[k, q].start()
    for k, q in order:
        slot = k * own + q
        first[k, q].wait_recv()
        mine = member(k, parity) * own + q
        if k == 0:
            out[q] = part[mine] + got[slot]
        else:
            summed[slot] = part[mine] + got[slot]
            second[k, q] = pltpu.make_async_remote_copy(
                src_ref=summed.at[slot],
                dst_ref=far.at[slot],
                send_sem=s2.at[slot],
                recv_sem=r2.at[slot],
                device_id={"tie": member(k, parity)},
                device_id_type=MESH,
            )
            second[k, q].start()
    for k, q in order:
        if k:
            second[k, q].wait_recv()
            out[q] += far[k * own + q]
    for k, q in order:
        first[k, q].wait_send()
        if k:
            second[k, q].wait_send()


def scatter_sum(partials, n):
    scenes, high, wide = partials.shape
    own = scenes // n
    slots = own * (n // 2)
    block = (slots, high, wide)
    dma = pltpu.SemaphoreType.DMA((slots,))
    return pl.pallas_call(
        functools.partial(scatter_kernel, n, own),
        out_shape=jax.ShapeDtypeStruct((own, high, wide), F32),
        in_specs=[VMEM],
        out_specs=VMEM,
        scratch_shapes=[pltpu.VMEM(block, F32)] * 3 + [dma] * 4,
        compiler_params=pltpu.CompilerParams(collective_id=0, has_side_effects=True),
        name="scatter",
    )(partials)


def three_parts(x):
    high = x.astype(BF16)
    rest = x - high.astype(F32)
    middle = rest.astype(BF16)
    return high, middle, (rest - middle.astype(F32)).astype(BF16)


def eliminate(panels, first_column):
    shape = panels[0].shape
    row_index = lax.broadcasted_iota(jnp.int32, shape, 0)
    lane = lax.broadcasted_iota(jnp.int32, shape, 1)
    for j in range(shape[0]):
        c = first_column + j
        for q, panel in enumerate(panels):
            column = jnp.broadcast_to(panel[:, c : c + 1], shape)
            scaled = panel[j : j + 1] / column[j : j + 1]
            panels[q] = panel - jnp.where(row_index > j, column, 0.0) * scaled
    above = lane >= row_index + first_column
    on_diagonal = lane == row_index + first_column
    done = []
    for panel in panels:
        diagonal = jnp.sum(jnp.where(on_diagonal, panel, 0.0), 1, keepdims=True)
        root = jnp.broadcast_to(jnp.sqrt(diagonal), shape)
        done.append(jnp.where(above, panel / root, 0.0))
    return done


def factor_kernel(damping, merged, sens, out, reduced, info):
    own, width, _ = info.shape
    spline = out.shape[1]
    half = width // 2
    row_index = lax.broadcasted_iota(jnp.int32, (width, width), 0)
    lane = lax.broadcasted_iota(jnp.int32, (width, width), 1)
    on_diagonal = (row_index == lane) & (row_index < spline)
    for q in range(own):
        side = merged[q, half : 2 * half]
        top = jnp.concatenate([merged[q, :half], side], 1)
        bottom = jnp.concatenate([side.T, merged[q, 2 * half :]], 1)
        whole = jnp.concatenate([top, bottom], 0)
        s = sens[q]
        mixed = whole
        for piece in three_parts(whole):
            mixed = mixed + jnp.dot(piece, s, preferred_element_type=F32)
        result = mixed + over_rows(s.astype(F32), mixed, HIGHEST)
        info[q] = result + jnp.where(on_diagonal, damping[q], 0.0)
    for start in range(0, spline, PANEL):
        base = start // LANES * LANES
        panels = [info[q, start : start + PANEL, base:] for q in range(own)]
        rows = eliminate(panels, start - base)
        for q in range(own):
            out[q, start : start + PANEL, base:] = rows[q]
        if base:
            out[:, start : start + PANEL, :base] = jnp.zeros((own, PANEL, base), F32)
        after = start + PANEL
        left = after // LANES * LANES
        for q in range(own):
            rest = rows[q][:, left - base :]
            info[q, after:, left:] -= over_rows(rest, rest, HIGHEST)[after - left :]
    total = info[0, spline:, half:]
    for q in range(1, own):
        total = total + info[q, spline:, half:]
    total = total[:, spline - half :]
    middle = (width - spline) // 2
    reduced[...] = jnp.concatenate([total[:middle], total[middle:]], 1)


def factor_scenes(merged, sensitivity, damping, width):
    own = damping.shape[0]
    spline = sensitivity.shape[1]
    half = width // 2
    mine = lax.dynamic_slice_in_dim(sensitivity, lax.axis_index("tie") * own, own)
    beyond = width - spline
    mine = jnp.pad(mine, ((0, 0), (0, beyond), (0, beyond)))
    return pl.pallas_call(
        factor_kernel,
        in_specs=[pl.BlockSpec(memory_space=pltpu.SMEM), VMEM, VMEM],
        out_specs=[VMEM, VMEM],
        scratch_shapes=[pltpu.VMEM((own, width, width), F32)],
        out_shape=[
            jax.ShapeDtypeStruct((own, spline, width), F32),
            jax.ShapeDtypeStruct(((width - spline) // 2, 2 * (width - spline)), F32),
        ],
        name="factor",
    )(damping, merged, mine)


def total_kernel(axes, x, out, *scratch):
    barrier = pltpu.get_barrier_semaphore()
    for name, n in axes:
        me = lax.axis_index(name)
        for k in range(1, n):
            pl.semaphore_signal(
                barrier, inc=1, device_id={name: lax.rem(me + k, n)}, device_id_type=MESH
            )
    pl.semaphore_wait(barrier, sum(n - 1 for _, n in axes))
    value = x
    for at, (name, n) in enumerate(axes):
        slots, send, recv = scratch[3 * at : 3 * at + 3]
        me = lax.axis_index(name)
        slots[0] = value[...]
        copies = []
        for k in range(1, n):
            copies.append(
                pltpu.make_async_remote_copy(
                    src_ref=slots.at[0],
                    dst_ref=slots.at[k],
                    send_sem=send.at[k],
                    recv_sem=recv.at[k],
                    device_id={name: lax.rem(me + k, n)},
                    device_id_type=MESH,
                )
            )
            copies[-1].start()
        for copy in copies:
            copy.wait_recv()
        acc = slots[me]
        for i in range(1, n):
            acc = acc + slots[lax.rem(me - i + n, n)]
        for copy in copies:
            copy.wait_send()
        out[...] = acc
        value = out


def total_sum(x, axes):
    scratch = []
    for _, n in axes:
        scratch += [pltpu.VMEM((n,) + x.shape, F32)]
        scratch += [pltpu.SemaphoreType.DMA((n,))] * 2
    return pl.pallas_call(
        functools.partial(total_kernel, axes),
        out_shape=jax.ShapeDtypeStruct(x.shape, F32),
        in_specs=[VMEM],
        out_specs=VMEM,
        scratch_shapes=scratch,
        compiler_params=pltpu.CompilerParams(collective_id=1, has_side_effects=True),
        name="total",
    )(x)


def last_kernel(scale, x, prior, out):
    shared = prior.shape[0]
    lane = lax.broadcasted_iota(jnp.int32, (shared, shared), 1)
    row = lax.broadcasted_iota(jnp.int32, (shared, shared), 0)
    packed = x[...]
    value = jnp.concatenate([packed[:, :shared], packed[:, shared:]], 0)
    value = value * scale + jnp.where(lane == row, prior[...], 0.0)
    out[...] = eliminate([value], 0)[0]


def last_factor(x, prior, scale):
    shared = prior.shape[0]
    return pl.pallas_call(
        functools.partial(last_kernel, scale),
        out_shape=jax.ShapeDtypeStruct((shared, shared), F32),
        in_specs=[VMEM, VMEM],
        out_specs=VMEM,
        name="last",
    )(x, prior[:, None])


def on_device(axes, tie_rows, point_counts, pattern, sensitivity, damping, prior):
    sizes = dict(axes)
    width = tie_rows.shape[2]
    partials = merged_partials(tie_rows, point_counts, pattern)
    merged = scatter_sum(partials, sizes["tie"])
    scene_rows, reduced = factor_scenes(merged, sensitivity, damping, width)
    total = total_sum(reduced, axes)
    scenes = damping.shape[0] * math.prod(sizes.values())
    return scene_rows, last_factor(total, prior, 1.0 / scenes)


def solution(mesh):
    axes = (("tie", mesh.shape["tie"]), ("scene", mesh.shape["scene"]))
    placed = (
        P("tie", None, None),
        P("tie"),
        P("scene", "tie"),
        P("scene", None, None),
        P(("scene", "tie")),
        P(),
    )
    return jax.shard_map(
        functools.partial(on_device, axes),
        mesh=mesh,
        in_specs=placed,
        out_specs=(P(("scene", "tie"), None, None), P()),
        check_vma=False,
    )
```
